256 devices in a mesh: row: 32 (over z, x_lo, core), col: 8 (over y, x_hi).
Axes of the slice: x: 4 (x_hi: 2, x_lo: 2; x = x_hi * 2 + x_lo), y: 4, z: 8, core: 2. Of those that a mesh axis runs over, the one named last changes fastest.
Arguments:
- x0_rows: bfloat16 [8192, 32768], P('row', 'col'), may hold values from -0.125 to 0.125
- x1_rows: bfloat16 [8192, 32768], P('row', 'col'), may hold values from -0.125 to 0.125
- x0_cols: bfloat16 [32768, 6144], P('row', 'col'), may hold values from -6 to 6
- x1_cols: bfloat16 [32768, 6144], P('row', 'col'), may hold values from -6 to 6
- mask0_rows: int32 [64, 256], P('row', 'col'), may hold values 0 or 1
- mask1_rows: int32 [64, 256], P('row', 'col'), may hold values 0 or 1
- mask0_cols: int32 [256, 48], P('row', 'col'), may hold values 0 or 1
- mask1_cols: int32 [256, 48], P('row', 'col'), may hold values 0 or 1
- keep_mask: int32 [64, 48], P('row', 'col'), may hold values 0 or 1
Outputs:
- x_square: bfloat16 [8192, 6144], P('row', 'col')
- x_tangent: bfloat16 [8192, 6144], P('row', 'col')
The draws below stay inside these ranges and needn't reach their ends.
All inputs are finite; a program needn't handle non-finite values. No bound on the sum of `mask0_rows` or of `mask1_rows` or of `mask0_cols` or of `mask1_cols` or of `keep_mask` on one device may be relied on, other than what follows from the above.
Results may differ from the reference program's by a relative error of at most 0.001.
Values may be sent and summed in bfloat16 or wider, within the bound.
A program may use at most 128 MiB of HBM per device.

```python
import jax
import jax.numpy as jnp

ORDER = 32768
BLOCK = 128
ROWS_DEV = 256
GROUP = 4
PANEL = 1024
WROWS = 8192
WCOLS = 6144
BLOCKS = 256
N_ROW = 32
N_COL = 8


def with_ends(entries, key, least, top_value):
    longest = entries.shape.index(max(entries.shape))
    spots = []
    for shift in (0, 1):
        where = [jax.random.randint(jax.random.fold_in(key, axis), (), 0, length) for axis, length in enumerate(entries.shape)]
        where[longest] = (where[longest] + shift) % entries.shape[longest]
        spots.append(tuple(where))
    return entries.at[spots[0]].set(least).at[spots[1]].set(top_value)


def steps_of(rng, dims, shards, smallest, largest):
    def one(position, blocks):
        heights = jax.random.uniform(jax.random.fold_in(jax.random.fold_in(rng, 6), position), (blocks,), jnp.float32, smallest / len(shards), largest / len(shards))
        return jnp.repeat(jnp.exp(heights), dims[position] // blocks).reshape((-1,) + (1,) * (len(dims) - position - 1))

    factor_of = one(*shards[0])
    for cut in shards[1:]:
        factor_of = factor_of * one(*cut)
    return factor_of


def normal_values(own_key, dims, spread, most, cuts=(), kind=jnp.bfloat16):
    level = steps_of(own_key, dims, cuts, -0.22, 0.18) if cuts else 1.0
    entries = jax.random.normal(own_key, dims, jnp.float32) * spread * level
    return jnp.minimum(jnp.maximum(entries, -most), most).astype(kind)


def setup_inputs(seed: int = 0) -> dict:
    arg_keys = jax.random.split(jax.random.key(seed), 10)
    return {
        "x0_rows": normal_values(arg_keys[0], (WROWS, ORDER), (ORDER * N_COL // (4 * N_ROW)) ** -0.5, 0.125, ((0, 32), (1, 8))),
        "x1_rows": normal_values(arg_keys[1], (WROWS, ORDER), (ORDER * N_COL // (4 * N_ROW)) ** -0.5, 0.125, ((0, 32), (1, 8))),
        "x0_cols": normal_values(arg_keys[2], (ORDER, WCOLS), 1.0, 6.0, ((0, 32), (1, 8))),
        "x1_cols": normal_values(arg_keys[3], (ORDER, WCOLS), 1.0, 6.0, ((0, 32), (1, 8))),
        "mask0_rows": with_ends((jax.random.randint(arg_keys[4], (WROWS // BLOCK, BLOCKS), 0, 2) < 1).astype(jnp.int32), jax.random.fold_in(arg_keys[4], 1), 0, 1),
        "mask1_rows": with_ends((jax.random.randint(arg_keys[5], (WROWS // BLOCK, BLOCKS), 0, 2) < 1).astype(jnp.int32), jax.random.fold_in(arg_keys[5], 1), 0, 1),
        "mask0_cols": with_ends((jax.random.randint(arg_keys[6], (BLOCKS, WCOLS // BLOCK), 0, 2) < 1).astype(jnp.int32), jax.random.fold_in(arg_keys[6], 1), 0, 1),
        "mask1_cols": with_ends((jax.random.randint(arg_keys[7], (BLOCKS, WCOLS // BLOCK), 0, 2) < 1).astype(jnp.int32), jax.random.fold_in(arg_keys[7], 1), 0, 1),
        "keep_mask": with_ends((jax.random.randint(arg_keys[8], (WROWS // BLOCK, WCOLS // BLOCK), 0, 4) < 3).astype(jnp.int32), jax.random.fold_in(arg_keys[8], 1), 0, 1),
    }


def masked(values, mask):
    rows_b, cols_b = mask.shape
    tiles = values.reshape(rows_b, BLOCK, cols_b, BLOCK)
    return (tiles * mask.astype(values.dtype)[:, None, :, None]).reshape(values.shape)


def pick_rows(left, which):
    shaped = left.reshape(N_COL, GROUP, ROWS_DEV, N_COL, GROUP, PANEL)
    return shaped[:, which, :, :, which, :].reshape(N_COL * ROWS_DEV, N_COL * PANEL)


def pick_cols(right, which):
    shaped = right.reshape(N_COL, GROUP, PANEL, WCOLS)
    return shaped[:, which].reshape(N_COL * PANEL, WCOLS)


def reference(x0_rows, x1_rows, x0_cols, x1_cols, mask0_rows, mask1_rows, mask0_cols, mask1_cols, keep_mask):
    left0 = masked(x0_rows, mask0_rows)
    left1 = masked(x1_rows, mask1_rows)
    right0 = masked(x0_cols, mask0_cols)
    right1 = masked(x1_cols, mask1_cols)
    squares = []
    tangents = []
    for which in range(GROUP):
        l_zero = pick_rows(left0, which)
        l_one = pick_rows(left1, which)
        r_zero = pick_cols(right0, which)
        r_one = pick_cols(right1, which)
        square = jnp.dot(l_zero, r_zero, preferred_element_type=jnp.float32)
        tangent = jnp.dot(l_zero, r_one, preferred_element_type=jnp.float32) + jnp.dot(l_one, r_zero, preferred_element_type=jnp.float32)
        squares.append(square.reshape(N_COL, ROWS_DEV, WCOLS))
        tangents.append(tangent.reshape(N_COL, ROWS_DEV, WCOLS))
    square_all = jnp.stack(squares, 1).reshape(WROWS, WCOLS)
    tangent_all = jnp.stack(tangents, 1).reshape(WROWS, WCOLS)
    x_square = masked(square_all, keep_mask).astype(jnp.bfloat16)
    x_tangent = masked(tangent_all, keep_mask).astype(jnp.bfloat16)
    return (x_square, x_tangent)
```

```python
import functools

import jax
import jax.numpy as jnp
from jax import lax
from jax.experimental import pallas as pl
from jax.experimental.pallas import tpu as pltpu
from jax.sharding import PartitionSpec as P

BLOCK = 128
LEVELS = 32760.0
FLOOR = 1e-33
MESH = pl.DeviceIdType.MESH


def kernel(
    group, nz, nc,
    x0_rows, x1_rows, x0_cols, x1_cols, m0_rows, m1_rows, m0_cols, m1_cols, keep,
    out_square, out_tangent,
    own, left, right, part, q_out, q_in, s_out, s_in, stage,
    load_sem, load_right_sem, v_send, left_recv, g_send, q_send, q_recv, s_send, s_recv, store_sem,
):
    rows, depth = own.shape[0] * own.shape[2], own.shape[3]
    piece = own.shape[2]
    cols = right.shape[2]
    half = part.shape[2]
    row = lax.axis_index("row")
    col = lax.axis_index("col")
    z, s = row // group, row % group
    y, xh = col // 2, col % 2
    ny = nc // 2
    partner = y * 2 + 1 - xh
    up_y, down_y = (y + 1) % ny, (y + ny - 1) % ny
    up, down = up_y * 2 + xh, down_y * 2 + xh
    on_diagonal = z == col

    def left_load(which, source, q):
        return pltpu.make_async_copy(
            source.at[pl.ds(q * piece, piece), pl.ds(pl.multiple_of(s * depth, depth), depth)],
            own.at[q, which],
            load_sem.at[which, q],
        )

    def right_load(which, source):
        return pltpu.make_async_copy(source, right.at[which], load_right_sem.at[which])

    for q in range(nc):
        left_load(0, x0_rows, q).start()
        left_load(1, x1_rows, q).start()
    right_load(0, x0_cols).start()
    right_load(1, x1_cols).start()

    barrier = pltpu.get_barrier_semaphore()
    for p in range(nz):

        @pl.when(jnp.logical_or(z != p, z != col))
        def _():
            pl.semaphore_signal(barrier, inc=1, device_id=(p * group + s, z), device_id_type=MESH)

    for c in (partner, up, down):
        pl.semaphore_signal(barrier, inc=1, device_id=(row, c), device_id_type=MESH)
    for zn in ((z + 1) % nz, (z + nz - 1) % nz):
        pl.semaphore_signal(barrier, inc=1, device_id=(zn * group + s, col), device_id_type=MESH)

    for q in range(nc):
        left_load(0, x0_rows, q).wait()
        left_load(1, x1_rows, q).wait()
        for which, mask in enumerate((m0_rows, m1_rows)):
            for j in range(depth // BLOCK):
                keep_it = mask[q * piece // BLOCK, s * (depth // BLOCK) + j].astype(jnp.float32)
                lanes = slice(j * BLOCK, (j + 1) * BLOCK)
                own[q, which, :, lanes] = (own[q, which, :, lanes].astype(jnp.float32) * keep_it).astype(jnp.bfloat16)

    pl.semaphore_wait(barrier, nz + 5 - jnp.where(on_diagonal, 1, 0))

    def scatter(q):
        return pltpu.make_async_remote_copy(
            src_ref=own.at[q],
            dst_ref=left.at[z, q],
            send_sem=v_send.at[q],
            recv_sem=left_recv.at[z, q],
            device_id=(col * group + s, q),
            device_id_type=MESH,
        )

    for q in range(nc):

        @pl.when(jnp.logical_or(z != col, col != q))
        def _():
            scatter(q).start()

    @pl.when(on_diagonal)
    def _():
        left[z, col] = own[col]

    right_load(0, x0_cols).wait()
    right_load(1, x1_cols).wait()

    @pl.loop(0, depth // BLOCK)
    def _(i):
        span = pl.ds(pl.multiple_of(i * BLOCK, BLOCK), BLOCK)
        for which, mask in enumerate((m0_cols, m1_cols)):
            for j in range(cols // BLOCK):
                keep_it = mask[i, j].astype(jnp.float32)
                lanes = slice(j * BLOCK, (j + 1) * BLOCK)
                right[which, span, lanes] = (right[which, span, lanes].astype(jnp.float32) * keep_it).astype(jnp.bfloat16)

    def distance(t):
        return nz // 2 - (t + 1) // 2

    def panel(t):
        ahead = t % 2
        return (z + ahead * distance(t) + (1 - ahead) * (nz - distance(t))) % nz

    def hand_on(t, q, c, k):
        p = panel(t)
        return pltpu.make_async_remote_copy(
            src_ref=left.at[p, q],
            dst_ref=left.at[p, q],
            send_sem=g_send.at[t, k],
            recv_sem=left_recv.at[p, q],
            device_id=(row, c),
            device_id_type=MESH,
        )

    def first(t):
        @pl.when(jnp.logical_or(panel(t) != z, z != col))
        def _():
            hand_on(t, col, partner, 0).wait_recv()

        hand_on(t, col, up, 1).start()
        hand_on(t, col, down, 2).start()
        hand_on(t, col, partner, 0).start()

    def second(t):
        hand_on(t, partner, partner, 0).wait_recv()
        hand_on(t, partner, up, 3).start()
        hand_on(t, partner, down, 4).start()

    from_down, from_up = down_y * 2, up_y * 2 + 1

    def third(t):
        hand_on(t, from_down, up, 5).wait_recv()
        hand_on(t, from_down, up, 5).start()
        hand_on(t, from_up, down, 6).wait_recv()
        hand_on(t, from_up, down, 6).start()

    far_y = (y + 2) % ny

    def rest(t):
        for q in (down_y * 2 + 1, up_y * 2, far_y * 2, far_y * 2 + 1):
            hand_on(t, q, up, 5).wait_recv()

    width = 256 if cols % 256 == 0 else BLOCK

    def products(t):
        p = panel(t)

        @pl.loop(0, cols // width)
        def _(n):
            start = pl.multiple_of(n * width, width)
            l0 = left[p, :, 0].reshape(rows, depth)
            l1 = left[p, :, 1].reshape(rows, depth)
            r0 = right[0, :, pl.ds(start, width)]
            r1 = right[1, :, pl.ds(start, width)]
            square = jnp.dot(l0, r0, preferred_element_type=jnp.float32)
            tangent = jnp.dot(l0, r1, preferred_element_type=jnp.float32)
            tangent = tangent + jnp.dot(l1, r0, preferred_element_type=jnp.float32)
            for h in range(2):
                part[t, h, :, pl.ds(start, width)] = square[h * half : (h + 1) * half]
                part[t, h, :, pl.ds(cols + start, width)] = tangent[h * half : (h + 1) * half]

    def slot_of(way, h, d):
        return (way * 2 + h) * (nz // 2) + d - 1

    def values_copy(way, h, d):
        slot = slot_of(way, h, d)
        zn = (z + 1 + way * (nz - 2)) % nz
        return pltpu.make_async_remote_copy(
            src_ref=q_out.at[slot],
            dst_ref=q_in.at[slot],
            send_sem=q_send.at[slot],
            recv_sem=q_recv.at[slot],
            device_id=(zn * group + s, col),
            device_id_type=MESH,
        )

    def scales_copy(way, h, d):
        slot = slot_of(way, h, d)
        zn = (z + 1 + way * (nz - 2)) % nz
        return pltpu.make_async_remote_copy(
            src_ref=s_out.at[slot],
            dst_ref=s_in.at[slot],
            send_sem=s_send.at[slot],
            recv_sem=s_recv.at[slot],
            device_id=(zn * group + s, col),
            device_id_type=MESH,
        )

    def arrived(way, h, d):
        values_copy(way, h, d).wait_recv()
        scales_copy(way, h, d).wait_recv()

    def decoded(slot, lanes):
        return q_in[slot, :, lanes].astype(jnp.int32).astype(jnp.float32) * s_in[slot, :, lanes]

    def send_on(t, way, h, d, adding):
        slot = slot_of(way, h, d)
        if adding:
            arrived(way, h, d + 1)

        @pl.loop(0, 2 * cols // BLOCK)
        def _(j):
            lanes = pl.ds(pl.multiple_of(j * BLOCK, BLOCK), BLOCK)
            total = part[t, h, :, lanes]
            if adding:
                total = total + decoded(slot + 1, lanes)
            top = jnp.maximum(jnp.max(jnp.abs(total), axis=0, keepdims=True), FLOOR)
            q_out[slot, :, lanes] = jnp.round(total * (LEVELS / top)).astype(jnp.int32).astype(jnp.int16)
            s_out[slot, :, lanes] = top * (1.0 / LEVELS)

        values_copy(way, h, d).start()
        scales_copy(way, h, d).start()

    first(0)
    first(1)
    first(2)
    second(0)
    second(1)
    third(0)

    @pl.loop(0, nz)
    def _(t):
        @pl.when(t + 3 < nz)
        def _():
            first(t + 3)

        @pl.when(t + 2 < nz)
        def _():
            second(t + 2)

        @pl.when(t + 1 < nz)
        def _():
            third(t + 1)

        rest(t)
        products(t)

        @pl.when(t == 0)
        def _():
            @pl.loop(0, 2)
            def _(way):
                send_on(t, way, way, nz // 2, False)

        @pl.when(jnp.logical_and(t > 0, t < nz - 1))
        def _():
            way = 1 - t % 2
            send_on(t, way, way, distance(t), True)

            @pl.when(t < 3)
            def _():
                send_on(t, way, 1 - way, distance(t), False)

            @pl.when(t >= 3)
            def _():
                send_on(t, way, 1 - way, distance(t), True)

    stores = []
    for h in range(2):
        arrived(0, h, 1)
        arrived(1, h, 1)
        for which in range(2):
            for j in range(cols // BLOCK):
                lanes = slice(which * cols + j * BLOCK, which * cols + (j + 1) * BLOCK)
                total = part[nz - 1, h, :, lanes] + decoded(slot_of(0, h, 1), lanes)
                total = total + decoded(slot_of(1, h, 1), lanes)
                keep_it = keep[h * half // BLOCK, j].astype(jnp.float32)
                stage[which, h, :, j * BLOCK : (j + 1) * BLOCK] = (total * keep_it).astype(jnp.bfloat16)
            out = (out_square, out_tangent)[which]
            store = pltpu.make_async_copy(stage.at[which, h], out.at[pl.ds(h * half, half)], store_sem.at[which, h])
            store.start()
            stores.append(store)

    for q in range(nc):

        @pl.when(jnp.logical_or(z != col, col != q))
        def _():
            scatter(q).wait_send()

    @pl.loop(0, nz)
    def _(t):
        for k, (q, c) in enumerate(
            ((col, partner), (col, up), (col, down), (partner, up), (partner, down), (from_down, up), (from_up, down))
        ):
            hand_on(t, q, c, k).wait_send()

    for way in range(2):
        for h in range(2):
            for d in range(1, nz // 2 + (1 if way == h else 0)):
                values_copy(way, h, d).wait_send()
                scales_copy(way, h, d).wait_send()
    for store in stores:
        store.wait()


def per_device(nz, nc, group, x0_rows, x1_rows, x0_cols, x1_cols, m0_rows, m1_rows, m0_cols, m1_cols, keep):
    rows = x0_rows.shape[0]
    depth, cols = x0_cols.shape
    piece, half, slots = rows // nc, rows // 2, 2 * nz
    hbm = pl.BlockSpec(memory_space=pl.ANY)
    smem = pl.BlockSpec(memory_space=pltpu.SMEM)
    dma = pltpu.SemaphoreType.DMA
    out = jax.ShapeDtypeStruct((rows, cols), jnp.bfloat16)
    return pl.pallas_call(
        functools.partial(kernel, group, nz, nc),
        out_shape=(out, out),
        in_specs=[hbm] * 4 + [smem] * 5,
        out_specs=(hbm, hbm),
        scratch_shapes=[
            pltpu.VMEM((nc, 2, piece, depth), jnp.bfloat16),
            pltpu.VMEM((nz, nc, 2, piece, depth), jnp.bfloat16),
            pltpu.VMEM((2, depth, cols), jnp.bfloat16),
            pltpu.VMEM((nz, 2, half, 2 * cols), jnp.float32),
            pltpu.VMEM((slots, half, 2 * cols), jnp.int16),
            pltpu.VMEM((slots, half, 2 * cols), jnp.int16),
            pltpu.VMEM((slots, 1, 2 * cols), jnp.float32),
            pltpu.VMEM((slots, 1, 2 * cols), jnp.float32),
            pltpu.VMEM((2, 2, half, cols), jnp.bfloat16),
            dma((2, nc)),
            dma((2,)),
            dma((nc,)),
            dma((nz, nc)),
            dma((nz, 7)),
            dma((slots,)),
            dma((slots,)),
            dma((slots,)),
            dma((slots,)),
            dma((2, 2)),
        ],
        compiler_params=pltpu.CompilerParams(
            collective_id=0, has_side_effects=True, vmem_limit_bytes=56 * 1024 * 1024
        ),
        name="window_kernel",
    )(x0_rows, x1_rows, x0_cols, x1_cols, m0_rows, m1_rows, m0_cols, m1_cols, keep)


def solution(mesh):
    nc = mesh.shape["col"]
    nz = 8
    group = mesh.shape["row"] // nz
    return jax.shard_map(
        functools.partial(per_device, nz, nc, group),
        mesh=mesh,
        in_specs=(P("row", "col"),) * 9,
        out_specs=(P("row", "col"), P("row", "col")),
        check_vma=False,
    )
```

```python
import functools

import jax
import jax.numpy as jnp
from jax import lax
from jax.experimental import pallas as pl
from jax.experimental.pallas import tpu as pltpu
from jax.sharding import PartitionSpec as P

BLOCK = 128
LEVELS = 32760.0
FLOOR = 1e-33
MESH = pl.DeviceIdType.MESH


def kernel(
    group, nz, nc,
    x0_rows, x1_rows, x0_cols, x1_cols, m0_rows, m1_rows, m0_cols, m1_cols, keep,
    out_square, out_tangent,
    own, middle, left, right, part, q_out, q_in, s_out, s_in, stage,
    load_sem, load_right_sem, v_send, v_recv, m_send, left_recv, g_send, q_send, q_recv, s_send, s_recv, store_sem,
):
    rows, depth = own.shape[0] * own.shape[2], own.shape[3]
    piece = own.shape[2]
    cols = right.shape[2]
    half = part.shape[2]
    row = lax.axis_index("row")
    col = lax.axis_index("col")
    z, s = row // group, row % group
    y, xh = col // 2, col % 2
    ny = nc // 2
    partner = y * 2 + 1 - xh
    up_y, down_y = (y + 1) % ny, (y + ny - 1) % ny
    up, down = up_y * 2 + xh, down_y * 2 + xh

    def left_load(which, source, q):
        return pltpu.make_async_copy(
            source.at[pl.ds(q * piece, piece), pl.ds(pl.multiple_of(s * depth, depth), depth)],
            own.at[q, which],
            load_sem.at[which, q],
        )

    def right_load(which, source):
        return pltpu.make_async_copy(source, right.at[which], load_right_sem.at[which])

    for q in range(nc):
        left_load(0, x0_rows, q).start()
        left_load(1, x1_rows, q).start()
    right_load(0, x0_cols).start()
    right_load(1, x1_cols).start()

    barrier = pltpu.get_barrier_semaphore()
    for i in range(1, nc):
        pl.semaphore_signal(barrier, inc=1, device_id=(row, (col + i) % nc), device_id_type=MESH)
    for i in range(1, nz):
        pl.semaphore_signal(barrier, inc=1, device_id=((z + i) % nz * group + s, col), device_id_type=MESH)

    for q in range(nc):
        left_load(0, x0_rows, q).wait()
        left_load(1, x1_rows, q).wait()
        for which, mask in enumerate((m0_rows, m1_rows)):
            for j in range(depth // BLOCK):
                keep_it = mask[q * piece // BLOCK, s * (depth // BLOCK) + j].astype(jnp.float32)
                lanes = slice(j * BLOCK, (j + 1) * BLOCK)
                own[q, which, :, lanes] = (own[q, which, :, lanes].astype(jnp.float32) * keep_it).astype(jnp.bfloat16)

    pl.semaphore_wait(barrier, nc + nz - 2)

    def scatter(i):
        q = (col + i) % nc
        return pltpu.make_async_remote_copy(
            src_ref=own.at[q],
            dst_ref=middle.at[col],
            send_sem=v_send.at[i],
            recv_sem=v_recv.at[col],
            device_id=(row, q),
            device_id_type=MESH,
        )

    def arrived_piece(j):
        return pltpu.make_async_remote_copy(
            src_ref=middle.at[j],
            dst_ref=middle.at[j],
            send_sem=v_send.at[0],
            recv_sem=v_recv.at[j],
            device_id=(row, j),
            device_id_type=MESH,
        )

    def to_plane(j):
        return pltpu.make_async_remote_copy(
            src_ref=middle.at[j],
            dst_ref=left.at[z, col],
            send_sem=m_send.at[j],
            recv_sem=left_recv.at[z, col, 0],
            device_id=(j * group + s, col),
            device_id_type=MESH,
        )

    for i in range(1, nc):
        scatter(i).start()
    middle[col] = own[col]

    @pl.when(z != col)
    def _():
        to_plane(col).start()


    right_load(0, x0_cols).wait()
    right_load(1, x1_cols).wait()

    @pl.loop(0, depth // BLOCK)
    def _(i):
        span = pl.ds(pl.multiple_of(i * BLOCK, BLOCK), BLOCK)
        for which, mask in enumerate((m0_cols, m1_cols)):
            for j in range(cols // BLOCK):
                keep_it = mask[i, j].astype(jnp.float32)
                lanes = slice(j * BLOCK, (j + 1) * BLOCK)
                right[which, span, lanes] = (right[which, span, lanes].astype(jnp.float32) * keep_it).astype(jnp.bfloat16)

    def onward(i):
        j = (z + i) % nz

        @pl.when(j != col)
        def _():
            arrived_piece(j).wait_recv()
            to_plane(j).start()

    onward(4)

    @pl.when(z != col)
    def _():
        arrived_piece(z).wait_recv()

    left[z, col] = middle[z]

    def distance(g):
        return nz // 2 - g // 2

    def panel(g):
        if isinstance(g, int) and g == 0:
            return z
        ahead = 1 - g % 2
        return (z + ahead * distance(g) + (1 - ahead) * (nz - distance(g))) % nz

    def hand_on(g, q, c, k, which=None):
        p = panel(g)
        ref = left.at[p, q] if which is None else left.at[p, q, which]
        return pltpu.make_async_remote_copy(
            src_ref=ref,
            dst_ref=ref,
            send_sem=g_send.at[g, k],
            recv_sem=left_recv.at[p, q, 0 if which is None else which],
            device_id=(row, c),
            device_id_type=MESH,
        )

    def wait_piece(g, q, which=None):
        hand_on(g, q, up, 0, which).wait_recv()

    far_y = (y + 2) % ny
    far, far_partner = far_y * 2 + xh, far_y * 2 + 1 - xh
    up_partner, down_partner = up_y * 2 + 1 - xh, down_y * 2 + 1 - xh
    from_down, from_up = down_y * 2, up_y * 2 + 1

    def first(g):
        if not (isinstance(g, int) and g == 0):
            wait_piece(g, col)
        hand_on(g, col, up, 0).start()
        hand_on(g, col, down, 1).start()
        hand_on(g, col, partner, 2).start()

    def second(g):
        turn = g // 2 % 2
        wait_piece(g, up)
        wait_piece(g, down)
        hand_on(g, down * turn + up * (1 - turn), up * turn + down * (1 - turn), 3, 1).start()
        hand_on(g, up, partner, 4, 1).start()
        hand_on(g, down, partner, 5, 1).start()
        wait_piece(g, partner)
        hand_on(g, partner, up, 6, 0).start()
        hand_on(g, partner, down, 7, 0).start()

    def third(g):
        wait_piece(g, far, 1)
        hand_on(g, far, partner, 8, 1).start()

        @pl.when(xh == 0)
        def _():
            wait_piece(g, up_partner, 0)

        @pl.when(xh == 1)
        def _():
            wait_piece(g, down_partner, 0)

        hand_on(g, from_down, up, 9, 0).start()
        hand_on(g, from_up, down, 10, 0).start()

    def rest(g):
        @pl.when(xh == 1)
        def _():
            wait_piece(g, up_partner, 0)

        @pl.when(xh == 0)
        def _():
            wait_piece(g, down_partner, 0)

        wait_piece(g, up_partner, 1)
        wait_piece(g, down_partner, 1)
        wait_piece(g, far, 0)
        wait_piece(g, far_partner, 0)
        wait_piece(g, far_partner, 1)

    width = 256 if cols % 256 == 0 else BLOCK

    def products(g):
        p = panel(g)

        @pl.loop(0, cols // width)
        def _(n):
            start = pl.multiple_of(n * width, width)
            l0 = left[p, :, 0].reshape(rows, depth)
            l1 = left[p, :, 1].reshape(rows, depth)
            r0 = right[0, :, pl.ds(start, width)]
            r1 = right[1, :, pl.ds(start, width)]
            square = jnp.dot(l0, r0, preferred_element_type=jnp.float32)
            tangent = jnp.dot(l0, r1, preferred_element_type=jnp.float32)
            tangent = tangent + jnp.dot(l1, r0, preferred_element_type=jnp.float32)
            for h in range(2):
                part[g, h, :, pl.ds(start, width)] = square[h * half : (h + 1) * half]
                part[g, h, :, pl.ds(cols + start, width)] = tangent[h * half : (h + 1) * half]

    def slot_of(way, h, d):
        return (way * 2 + h) * (nz // 2) + d - 1

    def values_copy(way, h, d):
        slot = slot_of(way, h, d)
        zn = (z + 1 + way * (nz - 2)) % nz
        return pltpu.make_async_remote_copy(
            src_ref=q_out.at[slot],
            dst_ref=q_in.at[slot],
            send_sem=q_send.at[slot],
            recv_sem=q_recv.at[slot],
            device_id=(zn * group + s, col),
            device_id_type=MESH,
        )

    def scales_copy(way, h, d):
        slot = slot_of(way, h, d)
        zn = (z + 1 + way * (nz - 2)) % nz
        return pltpu.make_async_remote_copy(
            src_ref=s_out.at[slot],
            dst_ref=s_in.at[slot],
            send_sem=s_send.at[slot],
            recv_sem=s_recv.at[slot],
            device_id=(zn * group + s, col),
            device_id_type=MESH,
        )

    def arrived(way, h, d):
        values_copy(way, h, d).wait_recv()
        scales_copy(way, h, d).wait_recv()

    def decoded(slot, lanes):
        return q_in[slot, :, lanes].astype(jnp.int32).astype(jnp.float32) * s_in[slot, :, lanes]

    def send_on(g, way, h, d, adding):
        slot = slot_of(way, h, d)
        if adding:
            arrived(way, h, d + 1)

        @pl.loop(0, 2 * cols // BLOCK)
        def _(j):
            lanes = pl.ds(pl.multiple_of(j * BLOCK, BLOCK), BLOCK)
            total = part[g, h, :, lanes]
            if adding:
                total = total + decoded(slot + 1, lanes)
            top = jnp.maximum(jnp.max(jnp.abs(total), axis=0, keepdims=True), FLOOR)
            q_out[slot, :, lanes] = jnp.round(total * (LEVELS / top)).astype(jnp.int32).astype(jnp.int16)
            s_out[slot, :, lanes] = top * (1.0 / LEVELS)

        values_copy(way, h, d).start()
        scales_copy(way, h, d).start()

    def stages(g):
        for lag, stage_of in zip((0, 1, 2), (third, second, first)):
            if isinstance(g, int):
                if g + lag >= 0:
                    stage_of(g + lag)
            else:
                pl.when(g + lag < nz)(functools.partial(stage_of, g + lag))

    stages(-2)
    onward(5)
    onward(3)
    stages(-1)
    onward(6)
    onward(2)
    stages(0)
    onward(7)
    onward(1)

    @pl.loop(1, nz)
    def _(g):
        stages(g)
        rest(g)
        products(g)

        @pl.when(g == 1)
        def _():
            @pl.loop(0, 2)
            def _(way):
                send_on(g, way, way, nz // 2, False)

        @pl.when(g > 1)
        def _():
            way = g % 2

            @pl.when(g < 4)
            def _():
                send_on(g, way, 1 - way, distance(g), False)

            @pl.when(g >= 4)
            def _():
                send_on(g, way, 1 - way, distance(g), True)

            send_on(g, way, way, distance(g), True)

    rest(0)
    products(0)

    stores = []
    for h in range(2):
        arrived(0, h, 1)
        arrived(1, h, 1)
        for which in range(2):
            for j in range(cols // BLOCK):
                lanes = slice(which * cols + j * BLOCK, which * cols + (j + 1) * BLOCK)
                total = part[0, h, :, lanes] + decoded(slot_of(0, h, 1), lanes)
                total = total + decoded(slot_of(1, h, 1), lanes)
                keep_it = keep[h * half // BLOCK, j].astype(jnp.float32)
                stage[which, h, :, j * BLOCK : (j + 1) * BLOCK] = (total * keep_it).astype(jnp.bfloat16)
            out = (out_square, out_tangent)[which]
            store = pltpu.make_async_copy(stage.at[which, h], out.at[pl.ds(h * half, half)], store_sem.at[which, h])
            store.start()
            stores.append(store)

    for i in range(1, nc):
        scatter(i).wait_send()
    for i in range(1, nz):
        to_plane((z + i) % nz).wait_send()

    def sent(g):
        for k in range(11):
            hand_on(g, col, up, k, None if k < 3 else 0).wait_send()

    sent(0)
    pl.loop(1, nz)(sent)

    for way in range(2):
        for h in range(2):
            for d in range(1, nz // 2 + (1 if way == h else 0)):
                values_copy(way, h, d).wait_send()
                scales_copy(way, h, d).wait_send()
    for store in stores:
        store.wait()


def per_device(nz, nc, group, x0_rows, x1_rows, x0_cols, x1_cols, m0_rows, m1_rows, m0_cols, m1_cols, keep):
    rows = x0_rows.shape[0]
    depth, cols = x0_cols.shape
    piece, half, slots = rows // nc, rows // 2, 2 * nz
    hbm = pl.BlockSpec(memory_space=pl.ANY)
    smem = pl.BlockSpec(memory_space=pltpu.SMEM)
    dma = pltpu.SemaphoreType.DMA
    out = jax.ShapeDtypeStruct((rows, cols), jnp.bfloat16)
    return pl.pallas_call(
        functools.partial(kernel, group, nz, nc),
        out_shape=(out, out),
        in_specs=[hbm] * 4 + [smem] * 5,
        out_specs=(hbm, hbm),
        scratch_shapes=[
            pltpu.VMEM((nc, 2, piece, depth), jnp.bfloat16),
            pltpu.VMEM((nc, 2, piece, depth), jnp.bfloat16),
            pltpu.VMEM((nz, nc, 2, piece, depth), jnp.bfloat16),
            pltpu.VMEM((2, depth, cols), jnp.bfloat16),
            pltpu.VMEM((nz, 2, half, 2 * cols), jnp.float32),
            pltpu.VMEM((slots, half, 2 * cols), jnp.int16),
            pltpu.VMEM((slots, half, 2 * cols), jnp.int16),
            pltpu.VMEM((slots, 1, 2 * cols), jnp.float32),
            pltpu.VMEM((slots, 1, 2 * cols), jnp.float32),
            pltpu.VMEM((2, 2, half, cols), jnp.bfloat16),
            dma((2, nc)),
            dma((2,)),
            dma((nc,)),
            dma((nc,)),
            dma((nz,)),
            dma((nz, nc, 2)),
            dma((nz, 11)),
            dma((slots,)),
            dma((slots,)),
            dma((slots,)),
            dma((slots,)),
            dma((2, 2)),
        ],
        compiler_params=pltpu.CompilerParams(
            collective_id=0, has_side_effects=True, vmem_limit_bytes=56 * 1024 * 1024
        ),
        name="window_kernel",
    )(x0_rows, x1_rows, x0_cols, x1_cols, m0_rows, m1_rows, m0_cols, m1_cols, keep)


def solution(mesh):
    nc = mesh.shape["col"]
    nz = 8
    group = mesh.shape["row"] // nz
    return jax.shard_map(
        functools.partial(per_device, nz, nc, group),
        mesh=mesh,
        in_specs=(P("row", "col"),) * 9,
        out_specs=(P("row", "col"), P("row", "col")),
        check_vma=False,
    )
```

```python
import functools

import jax
import jax.numpy as jnp
from jax import lax
from jax.experimental import pallas as pl
from jax.experimental.pallas import tpu as pltpu
from jax.sharding import PartitionSpec as P

BLOCK = 128
LEVELS = 32760.0
FLOOR = 1e-33
MESH = pl.DeviceIdType.MESH


def kernel(
    group, nz, nc,
    x0_rows, x1_rows, x0_cols, x1_cols, m0_rows, m1_rows, m0_cols, m1_cols, keep,
    out_square, out_tangent,
    own, middle, left, right, part, q_out, q_in, s_out, s_in, stage,
    load_sem, load_right_sem, v_send, v_recv, m_send, left_recv, g_send, q_send, q_recv, s_send, s_recv, store_sem,
):
    thin, depth = own.shape[3], own.shape[4]
    rows = nc * 2 * thin
    half = rows // 2
    cols = right.shape[2]
    row = lax.axis_index("row")
    col = lax.axis_index("col")
    z, s = row // group, row % group
    y, xh = col // 2, col % 2
    ny = nc // 2
    partner = y * 2 + 1 - xh
    up_y, down_y = (y + 1) % ny, (y + ny - 1) % ny
    up, down = up_y * 2 + xh, down_y * 2 + xh
    ahead = (col + nz - z) % nz

    barrier = pltpu.get_barrier_semaphore()
    for i in range(1, nc):
        pl.semaphore_signal(barrier, inc=1, device_id=(row, (col + i) % nc), device_id_type=MESH)
    for i in range(1, nz):
        pl.semaphore_signal(barrier, inc=1, device_id=((z + i) % nz * group + s, col), device_id_type=MESH)

    def left_load(which, source):
        return pltpu.make_async_copy(
            source.at[:, :, :, pl.ds(pl.multiple_of(s * depth, depth), depth)],
            own.at[:, :, which],
            load_sem.at[which],
        )

    def right_load(which, source):
        return pltpu.make_async_copy(source, right.at[which], load_right_sem.at[which])

    left_load(0, x0_rows).start()
    left_load(1, x1_rows).start()
    right_load(0, x0_cols).start()
    right_load(1, x1_cols).start()

    for which, (source, mask) in enumerate(((x0_rows, m0_rows), (x1_rows, m1_rows))):
        left_load(which, source).wait()
        for q in range(nc):
            for j in range(depth // BLOCK):
                keep_it = mask[q * 2 * thin // BLOCK, s * (depth // BLOCK) + j].astype(jnp.float32)
                lanes = slice(j * BLOCK, (j + 1) * BLOCK)
                own[q, :, which, :, lanes] = (own[q, :, which, :, lanes].astype(jnp.float32) * keep_it).astype(jnp.bfloat16)

    pl.semaphore_wait(barrier, nc + nz - 2)

    def copy_of(q, target, recv, k, device_row):
        return pltpu.make_async_remote_copy(
            src_ref=own.at[q],
            dst_ref=target,
            send_sem=v_send.at[k],
            recv_sem=recv,
            device_id=(device_row, q),
            device_id_type=MESH,
        )

    def scatter(k):
        q = (col + k) % nc
        return copy_of(q, middle.at[col], v_recv.at[col], k, row)

    def scatter_own(k):
        q = (col + k) % nc
        return copy_of(q, left.at[0, :, q], left_recv.at[0, q, 0], k, row)

    @pl.when(ahead == 0)
    def _():
        for k in range(1, nc):
            scatter_own(k).start()
        left[0, :, col] = own[col]

    @pl.when(ahead != 0)
    def _():
        for k in range(1, nc):
            scatter(k).start()
        middle[col] = own[col]

    def arrived_piece(j):
        return pltpu.make_async_remote_copy(
            src_ref=middle.at[j],
            dst_ref=middle.at[j],
            send_sem=v_send.at[0],
            recv_sem=v_recv.at[j],
            device_id=(row, j),
            device_id_type=MESH,
        )

    def to_plane(i, h):
        d = min(i, nz - i)
        if i == nz // 2:
            return pltpu.make_async_remote_copy(
                src_ref=middle.at[(z + i) % nz],
                dst_ref=left.at[1, :, col],
                send_sem=m_send.at[i, 0],
                recv_sem=left_recv.at[1, col, 0],
                device_id=((z + i) % nz * group + s, col),
                device_id_type=MESH,
            )
        u, b = 2 * (nz // 2 - d) + h, 1 if i < nz // 2 else 0
        j = (z + i) % nz
        return pltpu.make_async_remote_copy(
            src_ref=middle.at[j, h],
            dst_ref=left.at[u, b, col],
            send_sem=m_send.at[i, h],
            recv_sem=left_recv.at[u, col, b],
            device_id=(j * group + s, col),
            device_id_type=MESH,
        )

    for i in range(1, nz):

        @pl.when(ahead == i)
        def _():
            for h in range(1 if i == nz // 2 else 2):
                to_plane(i, h).start()

    right_load(0, x0_cols).wait()
    right_load(1, x1_cols).wait()

    @pl.loop(0, depth // BLOCK)
    def _(i):
        span = pl.ds(pl.multiple_of(i * BLOCK, BLOCK), BLOCK)
        for which, mask in enumerate((m0_cols, m1_cols)):
            for j in range(cols // BLOCK):
                keep_it = mask[i, j].astype(jnp.float32)
                lanes = slice(j * BLOCK, (j + 1) * BLOCK)
                right[which, span, lanes] = (right[which, span, lanes].astype(jnp.float32) * keep_it).astype(jnp.bfloat16)

    def onward(i, h):
        @pl.when(ahead != i)
        def _():
            if h == 0:
                arrived_piece((z + i) % nz).wait_recv()
            to_plane(i, h).start()

    def hand_on(u, q, c, k, which=None):
        ref = left.at[u, :, q] if which is None else left.at[u, :, q, which]
        return pltpu.make_async_remote_copy(
            src_ref=ref,
            dst_ref=ref,
            send_sem=g_send.at[u, k],
            recv_sem=left_recv.at[u, q, 0 if which is None else which],
            device_id=(row, c),
            device_id_type=MESH,
        )

    def wait_piece(u, q, which=None):
        hand_on(u, q, up, 0, which).wait_recv()

    def wait_half(u, b):
        pltpu.make_async_remote_copy(
            src_ref=left.at[u, b, col],
            dst_ref=left.at[u, b, col],
            send_sem=m_send.at[1, 0],
            recv_sem=left_recv.at[u, col, b],
            device_id=(row, up),
            device_id_type=MESH,
        ).wait_recv()

    far_y = (y + 2) % ny
    far, far_partner = far_y * 2 + xh, far_y * 2 + 1 - xh
    up_partner, down_partner = up_y * 2 + 1 - xh, down_y * 2 + 1 - xh
    from_down, from_up = down_y * 2, up_y * 2 + 1

    def first(u):
        if isinstance(u, int) and u == 0:

            @pl.when(ahead != 0)
            def _():
                wait_piece(u, col)

        elif isinstance(u, int) and u == 1:
            wait_piece(u, col)
        else:
            wait_half(u, 0)
            wait_half(u, 1)
        hand_on(u, col, up, 0).start()
        hand_on(u, col, down, 1).start()
        hand_on(u, col, partner, 2).start()

    def second(u):
        turn = u // 2 % 2
        wait_piece(u, up)
        wait_piece(u, down)
        hand_on(u, down * turn + up * (1 - turn), up * turn + down * (1 - turn), 3, 1).start()
        hand_on(u, up, partner, 4, 1).start()
        hand_on(u, down, partner, 5, 1).start()
        wait_piece(u, partner)
        hand_on(u, partner, up, 6, 0).start()
        hand_on(u, partner, down, 7, 0).start()

    def third(u):
        wait_piece(u, far, 1)
        hand_on(u, far, partner, 8, 1).start()

        @pl.when(xh == 0)
        def _():
            wait_piece(u, up_partner, 0)

        @pl.when(xh == 1)
        def _():
            wait_piece(u, down_partner, 0)

        hand_on(u, from_down, up, 9, 0).start()
        hand_on(u, from_up, down, 10, 0).start()

    def rest(u):
        @pl.when(xh == 1)
        def _():
            wait_piece(u, up_partner, 0)

        @pl.when(xh == 0)
        def _():
            wait_piece(u, down_partner, 0)

        wait_piece(u, up_partner, 1)
        wait_piece(u, down_partner, 1)
        wait_piece(u, far, 0)
        wait_piece(u, far_partner, 0)
        wait_piece(u, far_partner, 1)

    width = 256 if cols % 256 == 0 else BLOCK

    def products(u):

        @pl.loop(0, cols // width)
        def _(n):
            start = pl.multiple_of(n * width, width)
            l0 = left[u, :, :, 0].reshape(rows, depth)
            l1 = left[u, :, :, 1].reshape(rows, depth)
            r0 = right[0, :, pl.ds(start, width)]
            r1 = right[1, :, pl.ds(start, width)]
            square = jnp.dot(l0, r0, preferred_element_type=jnp.float32)
            tangent = jnp.dot(l0, r1, preferred_element_type=jnp.float32)
            tangent = tangent + jnp.dot(l1, r0, preferred_element_type=jnp.float32)
            for b in range(2):
                part[u, b, :, pl.ds(start, width)] = square[b * half : (b + 1) * half]
                part[u, b, :, pl.ds(cols + start, width)] = tangent[b * half : (b + 1) * half]

    def slot_of(way, h, d):
        return (way * 2 + h) * (nz // 2) + d - 1

    def values_copy(way, h, d):
        slot = slot_of(way, h, d)
        zn = (z + 1 + way * (nz - 2)) % nz
        return pltpu.make_async_remote_copy(
            src_ref=q_out.at[slot],
            dst_ref=q_in.at[slot],
            send_sem=q_send.at[slot],
            recv_sem=q_recv.at[slot],
            device_id=(zn * group + s, col),
            device_id_type=MESH,
        )

    def scales_copy(way, h, d):
        slot = slot_of(way, h, d)
        zn = (z + 1 + way * (nz - 2)) % nz
        return pltpu.make_async_remote_copy(
            src_ref=s_out.at[slot],
            dst_ref=s_in.at[slot],
            send_sem=s_send.at[slot],
            recv_sem=s_recv.at[slot],
            device_id=(zn * group + s, col),
            device_id_type=MESH,
        )

    def arrived(way, h, d):
        values_copy(way, h, d).wait_recv()
        scales_copy(way, h, d).wait_recv()

    def decoded(slot, lanes):
        return q_in[slot, :, lanes].astype(jnp.int32).astype(jnp.float32) * s_in[slot, :, lanes]

    def send_on(u, b, way, h, d, adding):
        slot = slot_of(way, h, d)
        if adding:
            arrived(way, h, d + 1)

        @pl.loop(0, 2 * cols // BLOCK)
        def _(j):
            lanes = pl.ds(pl.multiple_of(j * BLOCK, BLOCK), BLOCK)
            total = part[u, b, :, lanes]
            if adding:
                total = total + decoded(slot + 1, lanes)
            top = jnp.maximum(jnp.max(jnp.abs(total), axis=0, keepdims=True), FLOOR)
            q_out[slot, :, lanes] = jnp.round(total * (LEVELS / top)).astype(jnp.int32).astype(jnp.int16)
            s_out[slot, :, lanes] = top * (1.0 / LEVELS)

        values_copy(way, h, d).start()
        scales_copy(way, h, d).start()

    def ring_step(u):
        h, d = u % 2, nz // 2 - u // 2

        @pl.when(u < 4)
        def _():
            send_on(u, 1 - h, 1 - h, h, d, False)

        @pl.when(u >= 4)
        def _():
            send_on(u, 1 - h, 1 - h, h, d, True)

        send_on(u, h, h, h, d, True)

    def if_any(stage, u):
        pl.when(u < nz)(functools.partial(stage, u))

    onward(4, 0)
    first(0)
    onward(5, 0)
    onward(3, 0)
    second(0)
    first(1)
    onward(5, 1)
    onward(3, 1)
    onward(6, 0)
    onward(2, 0)
    third(0)
    second(1)
    first(2)
    onward(6, 1)
    onward(2, 1)
    onward(7, 0)
    onward(1, 0)
    onward(7, 1)
    onward(1, 1)
    third(1)
    second(2)
    first(3)
    rest(1)
    products(1)
    send_on(1, 0, 0, 0, nz // 2, False)
    send_on(1, 1, 1, 1, nz // 2, False)

    @pl.loop(2, nz)
    def _(u):
        third(u)
        if_any(second, u + 1)
        if_any(first, u + 2)
        rest(u)
        products(u)
        ring_step(u)

    rest(0)
    products(0)

    for h in range(2):
        arrived(0, h, 1)
        arrived(1, h, 1)
        for which in range(2):
            for j in range(cols // BLOCK):
                lanes = slice(which * cols + j * BLOCK, which * cols + (j + 1) * BLOCK)
                total = part[0, h, :, lanes] + decoded(slot_of(0, h, 1), lanes)
                total = total + decoded(slot_of(1, h, 1), lanes)
                total = total.reshape(nc, thin, BLOCK)
                per_block = BLOCK // (2 * thin)
                for i in range(nc // per_block):
                    keep_it = keep[i, j].astype(jnp.float32)
                    span = slice(i * per_block, (i + 1) * per_block)
                    stage[which, span, h, :, j * BLOCK : (j + 1) * BLOCK] = (total[span] * keep_it).astype(jnp.bfloat16)

    stores = []
    for which, out in enumerate((out_square, out_tangent)):
        store = pltpu.make_async_copy(stage.at[which], out, store_sem.at[which])
        store.start()
        stores.append(store)

    for k in range(1, nc):
        scatter(k).wait_send()
    for i in range(1, nz):
        for h in range(1 if i == nz // 2 else 2):
            to_plane(i, h).wait_send()

    def sent(u):
        for k in range(11):
            hand_on(u, col, up, k, None if k < 3 else 0).wait_send()

    pl.loop(0, nz)(sent)

    for way in range(2):
        for h in range(2):
            for d in range(1, nz // 2 + (1 if way == h else 0)):
                values_copy(way, h, d).wait_send()
                scales_copy(way, h, d).wait_send()
    for store in stores:
        store.wait()


def per_device(nz, nc, group, x0_rows, x1_rows, x0_cols, x1_cols, m0_rows, m1_rows, m0_cols, m1_cols, keep):
    rows = x0_rows.shape[0]
    depth, cols = x0_cols.shape
    thin, half, slots = rows // (2 * nc), rows // 2, 2 * nz
    x0_rows, x1_rows = (x.reshape(nc, 2, thin, -1) for x in (x0_rows, x1_rows))
    hbm = pl.BlockSpec(memory_space=pl.ANY)
    smem = pl.BlockSpec(memory_space=pltpu.SMEM)
    dma = pltpu.SemaphoreType.DMA
    out = jax.ShapeDtypeStruct((nc, 2, thin, cols), jnp.bfloat16)
    square, tangent = pl.pallas_call(
        functools.partial(kernel, group, nz, nc),
        out_shape=(out, out),
        in_specs=[hbm] * 4 + [smem] * 5,
        out_specs=(hbm, hbm),
        scratch_shapes=[
            pltpu.VMEM((nc, 2, 2, thin, depth), jnp.bfloat16),
            pltpu.VMEM((nc, 2, 2, thin, depth), jnp.bfloat16),
            pltpu.VMEM((nz, 2, nc, 2, thin, depth), jnp.bfloat16),
            pltpu.VMEM((2, depth, cols), jnp.bfloat16),
            pltpu.VMEM((nz, 2, half, 2 * cols), jnp.float32),
            pltpu.VMEM((slots, half, 2 * cols), jnp.int16),
            pltpu.VMEM((slots, half, 2 * cols), jnp.int16),
            pltpu.VMEM((slots, 1, 2 * cols), jnp.float32),
            pltpu.VMEM((slots, 1, 2 * cols), jnp.float32),
            pltpu.VMEM((2, nc, 2, thin, cols), jnp.bfloat16),
            dma((2,)),
            dma((2,)),
            dma((nc,)),
            dma((nc,)),
            dma((nz, 2)),
            dma((nz, nc, 2)),
            dma((nz, 11)),
            dma((slots,)),
            dma((slots,)),
            dma((slots,)),
            dma((slots,)),
            dma((2,)),
        ],
        compiler_params=pltpu.CompilerParams(
            collective_id=0, has_side_effects=True, vmem_limit_bytes=56 * 1024 * 1024
        ),
        name="window_kernel",
    )(x0_rows, x1_rows, x0_cols, x1_cols, m0_rows, m1_rows, m0_cols, m1_cols, keep)
    return square.reshape(rows, cols), tangent.reshape(rows, cols)


def solution(mesh):
    nc = mesh.shape["col"]
    nz = 8
    group = mesh.shape["row"] // nz
    return jax.shard_map(
        functools.partial(per_device, nz, nc, group),
        mesh=mesh,
        in_specs=(P("row", "col"),) * 9,
        out_specs=(P("row", "col"), P("row", "col")),
        check_vma=False,
    )
```

```python
import functools

import jax
import jax.numpy as jnp
from jax import lax
from jax.experimental import pallas as pl
from jax.experimental.pallas import tpu as pltpu
from jax.sharding import PartitionSpec as P

BLOCK = 128
LEVELS = 32760.0
FLOOR = 1e-33
MESH = pl.DeviceIdType.MESH


def kernel(
    group, nz, nc,
    x0_rows, x1_rows, x0_cols, x1_cols, m0_rows, m1_rows, m0_cols, m1_cols, keep,
    out_square, out_tangent,
    own, middle, left, right, part, q_out, q_in, s_out, s_in, stage,
    load_sem, load_right_sem, v_send, v_recv, m_send, left_recv, g_send, q_send, q_recv, s_send, s_recv, store_sem,
):
    thin, depth = own.shape[3], own.shape[4]
    rows = nc * 2 * thin
    half = rows // 2
    cols = right.shape[2]
    row = lax.axis_index("row")
    col = lax.axis_index("col")
    z, s = row // group, row % group
    y, xh = col // 2, col % 2
    ny = nc // 2
    partner = y * 2 + 1 - xh
    up_y, down_y = (y + 1) % ny, (y + ny - 1) % ny
    up, down = up_y * 2 + xh, down_y * 2 + xh
    ahead = (col + nz - z) % nz

    barrier = pltpu.get_barrier_semaphore()
    for i in range(1, nz):
        pl.semaphore_signal(barrier, inc=1, device_id=((z + i) % nz * group + s, col), device_id_type=MESH)
    for i in range(1, nc):
        pl.semaphore_signal(barrier, inc=1, device_id=(row, (col + i) % nc), device_id_type=MESH)

    def left_load(which, source):
        return pltpu.make_async_copy(
            source.at[:, :, :, pl.ds(pl.multiple_of(s * depth, depth), depth)],
            own.at[:, :, which],
            load_sem.at[which],
        )

    def right_load(which, source):
        return pltpu.make_async_copy(source, right.at[which], load_right_sem.at[which])

    left_load(0, x0_rows).start()
    left_load(1, x1_rows).start()
    right_load(0, x0_cols).start()
    right_load(1, x1_cols).start()

    for which, (source, mask) in enumerate(((x0_rows, m0_rows), (x1_rows, m1_rows))):
        left_load(which, source).wait()
        for q in range(nc):
            for j in range(depth // BLOCK):
                keep_it = mask[q * 2 * thin // BLOCK, s * (depth // BLOCK) + j].astype(jnp.float32)
                lanes = slice(j * BLOCK, (j + 1) * BLOCK)
                own[q, :, which, :, lanes] = (own[q, :, which, :, lanes].astype(jnp.float32) * keep_it).astype(jnp.bfloat16)

    pl.semaphore_wait(barrier, nc + nz - 2)

    def copy_of(q, target, recv, k, device_row):
        return pltpu.make_async_remote_copy(
            src_ref=own.at[q],
            dst_ref=target,
            send_sem=v_send.at[k],
            recv_sem=recv,
            device_id=(device_row, q),
            device_id_type=MESH,
        )

    def scatter(k):
        q = (col + k) % nc
        return copy_of(q, middle.at[col], v_recv.at[col], k, row)

    def scatter_own(k):
        q = (col + k) % nc
        return copy_of(q, left.at[0, :, q], left_recv.at[0, q, 0], k, row)

    @pl.when(ahead == 0)
    def _():
        for k in range(1, nc):
            scatter_own(k).start()
        left[0, :, col] = own[col]

    @pl.when(ahead != 0)
    def _():
        for k in range(1, nc):
            scatter(k).start()
        middle[col] = own[col]

    def arrived_piece(j):
        return pltpu.make_async_remote_copy(
            src_ref=middle.at[j],
            dst_ref=middle.at[j],
            send_sem=v_send.at[0],
            recv_sem=v_recv.at[j],
            device_id=(row, j),
            device_id_type=MESH,
        )

    def to_plane(i, h):
        d = min(i, nz - i)
        if i == nz // 2:
            return pltpu.make_async_remote_copy(
                src_ref=middle.at[(z + i) % nz],
                dst_ref=left.at[1, :, col],
                send_sem=m_send.at[i, 0],
                recv_sem=left_recv.at[1, col, 0],
                device_id=((z + i) % nz * group + s, col),
                device_id_type=MESH,
            )
        u, b = 2 * (nz // 2 - d) + h, 1 if i < nz // 2 else 0
        j = (z + i) % nz
        return pltpu.make_async_remote_copy(
            src_ref=middle.at[j, h],
            dst_ref=left.at[u, b, col],
            send_sem=m_send.at[i, h],
            recv_sem=left_recv.at[u, col, b],
            device_id=(j * group + s, col),
            device_id_type=MESH,
        )

    for i in range(1, nz):

        @pl.when(ahead == i)
        def _():
            for h in range(1 if i == nz // 2 else 2):
                to_plane(i, h).start()

    right_load(0, x0_cols).wait()
    right_load(1, x1_cols).wait()

    @pl.loop(0, depth // BLOCK)
    def _(i):
        span = pl.ds(pl.multiple_of(i * BLOCK, BLOCK), BLOCK)
        for which, mask in enumerate((m0_cols, m1_cols)):
            for j in range(cols // BLOCK):
                keep_it = mask[i, j].astype(jnp.float32)
                lanes = slice(j * BLOCK, (j + 1) * BLOCK)
                right[which, span, lanes] = (right[which, span, lanes].astype(jnp.float32) * keep_it).astype(jnp.bfloat16)

    def onward(i, h):
        @pl.when(ahead != i)
        def _():
            if h == 0:
                arrived_piece((z + i) % nz).wait_recv()
            to_plane(i, h).start()

    def hand_on(u, q, c, k, which=None):
        ref = left.at[u, :, q] if which is None else left.at[u, :, q, which]
        return pltpu.make_async_remote_copy(
            src_ref=ref,
            dst_ref=ref,
            send_sem=g_send.at[u, k],
            recv_sem=left_recv.at[u, q, 0 if which is None else which],
            device_id=(row, c),
            device_id_type=MESH,
        )

    def wait_piece(u, q, which=None):
        hand_on(u, q, up, 0, which).wait_recv()

    def wait_half(u, b):
        pltpu.make_async_remote_copy(
            src_ref=left.at[u, b, col],
            dst_ref=left.at[u, b, col],
            send_sem=m_send.at[1, 0],
            recv_sem=left_recv.at[u, col, b],
            device_id=(row, up),
            device_id_type=MESH,
        ).wait_recv()

    far_y = (y + 2) % ny
    far, far_partner = far_y * 2 + xh, far_y * 2 + 1 - xh
    up_partner, down_partner = up_y * 2 + 1 - xh, down_y * 2 + 1 - xh
    from_down, from_up = down_y * 2, up_y * 2 + 1

    def first(u):
        if isinstance(u, int) and u == 0:

            @pl.when(ahead != 0)
            def _():
                wait_piece(u, col)

        elif isinstance(u, int) and u == 1:
            wait_piece(u, col)
        else:
            wait_half(u, 0)
            wait_half(u, 1)
        hand_on(u, col, up, 0).start()
        hand_on(u, col, down, 1).start()
        hand_on(u, col, partner, 2).start()

    def second(u):
        turn = u // 2 % 2
        wait_piece(u, up)
        wait_piece(u, down)
        hand_on(u, down * turn + up * (1 - turn), up * turn + down * (1 - turn), 3, 1).start()
        hand_on(u, up, partner, 4, 1).start()
        hand_on(u, down, partner, 5, 1).start()
        wait_piece(u, partner)
        hand_on(u, partner, up, 6, 0).start()
        hand_on(u, partner, down, 7, 0).start()

    def third(u):
        wait_piece(u, far, 1)
        hand_on(u, far, partner, 8, 1).start()

        @pl.when(xh == 0)
        def _():
            wait_piece(u, up_partner, 0)

        @pl.when(xh == 1)
        def _():
            wait_piece(u, down_partner, 0)

        hand_on(u, from_down, up, 9, 0).start()
        hand_on(u, from_up, down, 10, 0).start()

    def rest(u):
        @pl.when(xh == 1)
        def _():
            wait_piece(u, up_partner, 0)

        @pl.when(xh == 0)
        def _():
            wait_piece(u, down_partner, 0)

        wait_piece(u, up_partner, 1)
        wait_piece(u, down_partner, 1)
        wait_piece(u, far, 0)
        wait_piece(u, far_partner, 0)
        wait_piece(u, far_partner, 1)

    width = 256 if cols % 256 == 0 else BLOCK

    def products(u):

        @pl.loop(0, cols // width)
        def _(n):
            start = pl.multiple_of(n * width, width)
            l0 = left[u, :, :, 0].reshape(rows, depth)
            l1 = left[u, :, :, 1].reshape(rows, depth)
            r0 = right[0, :, pl.ds(start, width)]
            r1 = right[1, :, pl.ds(start, width)]
            square = jnp.dot(l0, r0, preferred_element_type=jnp.float32)
            tangent = jnp.dot(l0, r1, preferred_element_type=jnp.float32)
            tangent = tangent + jnp.dot(l1, r0, preferred_element_type=jnp.float32)
            for b in range(2):
                part[u, b, :, pl.ds(start, width)] = square[b * half : (b + 1) * half]
                part[u, b, :, pl.ds(cols + start, width)] = tangent[b * half : (b + 1) * half]

    def slot_of(way, h, d):
        return (way * 2 + h) * (nz // 2) + d - 1

    def values_copy(way, h, d):
        slot = slot_of(way, h, d)
        zn = (z + 1 + way * (nz - 2)) % nz
        return pltpu.make_async_remote_copy(
            src_ref=q_out.at[slot],
            dst_ref=q_in.at[slot],
            send_sem=q_send.at[slot],
            recv_sem=q_recv.at[slot],
            device_id=(zn * group + s, col),
            device_id_type=MESH,
        )

    def scales_copy(way, h, d):
        slot = slot_of(way, h, d)
        zn = (z + 1 + way * (nz - 2)) % nz
        return pltpu.make_async_remote_copy(
            src_ref=s_out.at[slot],
            dst_ref=s_in.at[slot],
            send_sem=s_send.at[slot],
            recv_sem=s_recv.at[slot],
            device_id=(zn * group + s, col),
            device_id_type=MESH,
        )

    def arrived(way, h, d):
        values_copy(way, h, d).wait_recv()
        scales_copy(way, h, d).wait_recv()

    def decoded(slot, lanes):
        return q_in[slot, :, lanes].astype(jnp.int32).astype(jnp.float32) * s_in[slot, :, lanes]

    def send_on(u, b, way, h, d, adding):
        slot = slot_of(way, h, d)
        if adding:
            arrived(way, h, d + 1)

        @pl.loop(0, 2 * cols // BLOCK)
        def _(j):
            lanes = pl.ds(pl.multiple_of(j * BLOCK, BLOCK), BLOCK)
            total = part[u, b, :, lanes]
            if adding:
                total = total + decoded(slot + 1, lanes)
            top = jnp.maximum(jnp.max(jnp.abs(total), axis=0, keepdims=True), FLOOR)
            q_out[slot, :, lanes] = jnp.round(total * (LEVELS / top)).astype(jnp.int32).astype(jnp.int16)
            s_out[slot, :, lanes] = top * (1.0 / LEVELS)

        values_copy(way, h, d).start()
        scales_copy(way, h, d).start()

    def ring_step(u):
        h, d = u % 2, nz // 2 - u // 2

        @pl.when(u < 4)
        def _():
            send_on(u, 1 - h, 1 - h, h, d, False)

        @pl.when(u >= 4)
        def _():
            send_on(u, 1 - h, 1 - h, h, d, True)

        send_on(u, h, h, h, d, True)

    def if_any(stage, u):
        pl.when(u < nz)(functools.partial(stage, u))

    onward(4, 0)
    first(0)
    second(0)
    first(1)
    onward(5, 0)
    onward(3, 0)
    second(1)
    onward(5, 1)
    onward(3, 1)
    third(1)
    onward(6, 0)
    onward(2, 0)
    onward(6, 1)
    onward(2, 1)
    first(2)
    rest(1)
    products(1)
    send_on(1, 0, 0, 0, nz // 2, False)
    send_on(1, 1, 1, 1, nz // 2, False)
    second(2)
    first(3)
    third(0)
    onward(7, 0)
    onward(1, 0)
    onward(7, 1)
    onward(1, 1)

    @pl.loop(2, nz)
    def _(u):
        third(u)
        if_any(second, u + 1)
        if_any(first, u + 2)
        rest(u)
        products(u)
        ring_step(u)

    rest(0)
    products(0)

    for h in range(2):
        arrived(0, h, 1)
        arrived(1, h, 1)
        for which in range(2):
            for j in range(cols // BLOCK):
                lanes = slice(which * cols + j * BLOCK, which * cols + (j + 1) * BLOCK)
                total = part[0, h, :, lanes] + decoded(slot_of(0, h, 1), lanes)
                total = total + decoded(slot_of(1, h, 1), lanes)
                total = total.reshape(nc, thin, BLOCK)
                per_block = BLOCK // (2 * thin)
                for i in range(nc // per_block):
                    keep_it = keep[i, j].astype(jnp.float32)
                    span = slice(i * per_block, (i + 1) * per_block)
                    stage[which, span, h, :, j * BLOCK : (j + 1) * BLOCK] = (total[span] * keep_it).astype(jnp.bfloat16)

    stores = []
    for which, out in enumerate((out_square, out_tangent)):
        store = pltpu.make_async_copy(stage.at[which], out, store_sem.at[which])
        store.start()
        stores.append(store)

    for k in range(1, nc):
        scatter(k).wait_send()
    for i in range(1, nz):
        for h in range(1 if i == nz // 2 else 2):
            to_plane(i, h).wait_send()

    def sent(u):
        for k in range(11):
            hand_on(u, col, up, k, None if k < 3 else 0).wait_send()

    pl.loop(0, nz)(sent)

    for way in range(2):
        for h in range(2):
            for d in range(1, nz // 2 + (1 if way == h else 0)):
                values_copy(way, h, d).wait_send()
                scales_copy(way, h, d).wait_send()
    for store in stores:
        store.wait()


def hand_out(square, tangent, out_square, out_tangent):
    out_square[...] = square[...]
    out_tangent[...] = tangent[...]


def per_device(nz, nc, group, x0_rows, x1_rows, x0_cols, x1_cols, m0_rows, m1_rows, m0_cols, m1_cols, keep):
    rows = x0_rows.shape[0]
    depth, cols = x0_cols.shape
    thin, half, slots = rows // (2 * nc), rows // 2, 2 * nz
    x0_rows, x1_rows = (x.reshape(nc, 2, thin, -1) for x in (x0_rows, x1_rows))
    hbm = pl.BlockSpec(memory_space=pl.ANY)
    smem = pl.BlockSpec(memory_space=pltpu.SMEM)
    dma = pltpu.SemaphoreType.DMA
    out = jax.ShapeDtypeStruct((nc, 2, thin, cols), jnp.bfloat16)
    square, tangent = pl.pallas_call(
        functools.partial(kernel, group, nz, nc),
        out_shape=(out, out),
        in_specs=[hbm] * 4 + [smem] * 5,
        out_specs=(hbm, hbm),
        scratch_shapes=[
            pltpu.VMEM((nc, 2, 2, thin, depth), jnp.bfloat16),
            pltpu.VMEM((nc, 2, 2, thin, depth), jnp.bfloat16),
            pltpu.VMEM((nz, 2, nc, 2, thin, depth), jnp.bfloat16),
            pltpu.VMEM((2, depth, cols), jnp.bfloat16),
            pltpu.VMEM((nz, 2, half, 2 * cols), jnp.float32),
            pltpu.VMEM((slots, half, 2 * cols), jnp.int16),
            pltpu.VMEM((slots, half, 2 * cols), jnp.int16),
            pltpu.VMEM((slots, 1, 2 * cols), jnp.float32),
            pltpu.VMEM((slots, 1, 2 * cols), jnp.float32),
            pltpu.VMEM((2, nc, 2, thin, cols), jnp.bfloat16),
            dma((2,)),
            dma((2,)),
            dma((nc,)),
            dma((nc,)),
            dma((nz, 2)),
            dma((nz, nc, 2)),
            dma((nz, 11)),
            dma((slots,)),
            dma((slots,)),
            dma((slots,)),
            dma((slots,)),
            dma((2,)),
        ],
        compiler_params=pltpu.CompilerParams(
            collective_id=0, has_side_effects=True, vmem_limit_bytes=56 * 1024 * 1024
        ),
        name="window_kernel",
    )(x0_rows, x1_rows, x0_cols, x1_cols, m0_rows, m1_rows, m0_cols, m1_cols, keep)
    return pl.pallas_call(
        hand_out,
        out_shape=(jax.ShapeDtypeStruct((rows, cols), jnp.bfloat16),) * 2,
        name="hand_out",
    )(square.reshape(rows, cols), tangent.reshape(rows, cols))


def solution(mesh):
    nc = mesh.shape["col"]
    nz = 8
    group = mesh.shape["row"] // nz
    return jax.shard_map(
        functools.partial(per_device, nz, nc, group),
        mesh=mesh,
        in_specs=(P("row", "col"),) * 9,
        out_specs=(P("row", "col"), P("row", "col")),
        check_vma=False,
    )
```

```python
import functools

import jax
import jax.numpy as jnp
from jax import lax
from jax.experimental import pallas as pl
from jax.experimental.pallas import tpu as pltpu
from jax.sharding import PartitionSpec as P

BLOCK = 128
LEVELS = 32760.0
FLOOR = 1e-33
MESH = pl.DeviceIdType.MESH


def kernel(
    group, nz, nc,
    x0_rows, x1_rows, x0_cols, x1_cols, m0_rows, m1_rows, m0_cols, m1_cols, keep,
    out_square, out_tangent,
    own, middle, left, right, part, q_out, q_in, s_out, s_in, stage,
    load_sem, load_right_sem, v_send, v_recv, m_send, left_recv, g_send, q_send, q_recv, s_send, s_recv, store_sem,
):
    thin, depth = own.shape[3], own.shape[4]
    rows = nc * 2 * thin
    half = rows // 2
    cols = right.shape[2]
    row = lax.axis_index("row")
    col = lax.axis_index("col")
    z, s = row // group, row % group
    y, xh = col // 2, col % 2
    ny = nc // 2
    partner = y * 2 + 1 - xh
    up_y, down_y = (y + 1) % ny, (y + ny - 1) % ny
    up, down = up_y * 2 + xh, down_y * 2 + xh
    ahead = (col + nz - z) % nz

    barrier = pltpu.get_barrier_semaphore()
    for i in range(1, nz):
        pl.semaphore_signal(barrier, inc=1, device_id=((z + i) % nz * group + s, col), device_id_type=MESH)
    for i in range(1, nc):
        pl.semaphore_signal(barrier, inc=1, device_id=(row, (col + i) % nc), device_id_type=MESH)

    def left_load(which, source):
        return pltpu.make_async_copy(
            source.at[:, :, :, pl.ds(pl.multiple_of(s * depth, depth), depth)],
            own.at[:, :, which],
            load_sem.at[which],
        )

    def right_load(which, source):
        return pltpu.make_async_copy(source, right.at[which], load_right_sem.at[which])

    left_load(0, x0_rows).start()
    left_load(1, x1_rows).start()
    right_load(0, x0_cols).start()
    right_load(1, x1_cols).start()

    for which, (source, mask) in enumerate(((x0_rows, m0_rows), (x1_rows, m1_rows))):
        left_load(which, source).wait()
        for q in range(nc):
            for j in range(depth // BLOCK):
                keep_it = mask[q * 2 * thin // BLOCK, s * (depth // BLOCK) + j].astype(jnp.float32)
                lanes = slice(j * BLOCK, (j + 1) * BLOCK)
                own[q, :, which, :, lanes] = (own[q, :, which, :, lanes].astype(jnp.float32) * keep_it).astype(jnp.bfloat16)

    pl.semaphore_wait(barrier, nc + nz - 2)

    def copy_of(q, target, recv, k, device_row):
        return pltpu.make_async_remote_copy(
            src_ref=own.at[q],
            dst_ref=target,
            send_sem=v_send.at[k],
            recv_sem=recv,
            device_id=(device_row, q),
            device_id_type=MESH,
        )

    def scatter(k):
        q = (col + k) % nc
        return copy_of(q, middle.at[col], v_recv.at[col], k, row)

    def scatter_own(k):
        q = (col + k) % nc
        return copy_of(q, left.at[0, :, q], left_recv.at[0, q, 0], k, row)

    def arrived_piece(j):
        return pltpu.make_async_remote_copy(
            src_ref=middle.at[j],
            dst_ref=middle.at[j],
            send_sem=v_send.at[0],
            recv_sem=v_recv.at[j],
            device_id=(row, j),
            device_id_type=MESH,
        )

    def to_plane(i, h):
        d = min(i, nz - i)
        if i == nz // 2:
            return pltpu.make_async_remote_copy(
                src_ref=middle.at[(z + i) % nz],
                dst_ref=left.at[1, :, col],
                send_sem=m_send.at[i, 0],
                recv_sem=left_recv.at[1, col, 0],
                device_id=((z + i) % nz * group + s, col),
                device_id_type=MESH,
            )
        u, b = 2 * (nz // 2 - d) + h, 1 if i < nz // 2 else 0
        j = (z + i) % nz
        return pltpu.make_async_remote_copy(
            src_ref=middle.at[j, h],
            dst_ref=left.at[u, b, col],
            send_sem=m_send.at[i, h],
            recv_sem=left_recv.at[u, col, b],
            device_id=(j * group + s, col),
            device_id_type=MESH,
        )

    def mask_right(i):
        span = pl.ds(pl.multiple_of(i * BLOCK, BLOCK), BLOCK)
        for which, mask in enumerate((m0_cols, m1_cols)):
            for j in range(cols // BLOCK):
                keep_it = mask[i, j].astype(jnp.float32)
                lanes = slice(j * BLOCK, (j + 1) * BLOCK)
                right[which, span, lanes] = (right[which, span, lanes].astype(jnp.float32) * keep_it).astype(jnp.bfloat16)

    def scatter_all():
        for k in range(1, nc):
            scatter(k).start()
        middle[col] = own[col]

    @pl.when(ahead == nz // 2)
    def _():
        scatter_all()
        to_plane(nz // 2, 0).start()

    right_load(0, x0_cols).wait()
    right_load(1, x1_cols).wait()
    pl.loop(0, 4)(mask_right)

    @pl.when(ahead == 0)
    def _():
        for k in range(1, nc):
            scatter_own(k).start()
        left[0, :, col] = own[col]

    @pl.when(ahead % (nz // 2) != 0)
    def _():
        scatter_all()

    for i in range(1, nz):
        if i != nz // 2:

            @pl.when(ahead == i)
            def _():
                for h in range(2):
                    to_plane(i, h).start()

    pl.loop(4, depth // BLOCK)(mask_right)

    def onward(i, h):
        @pl.when(ahead != i)
        def _():
            if h == 0:
                arrived_piece((z + i) % nz).wait_recv()
            to_plane(i, h).start()

    def hand_on(u, q, c, k, which=None):
        ref = left.at[u, :, q] if which is None else left.at[u, :, q, which]
        return pltpu.make_async_remote_copy(
            src_ref=ref,
            dst_ref=ref,
            send_sem=g_send.at[u, k],
            recv_sem=left_recv.at[u, q, 0 if which is None else which],
            device_id=(row, c),
            device_id_type=MESH,
        )

    def wait_piece(u, q, which=None):
        hand_on(u, q, up, 0, which).wait_recv()

    def wait_half(u, b):
        pltpu.make_async_remote_copy(
            src_ref=left.at[u, b, col],
            dst_ref=left.at[u, b, col],
            send_sem=m_send.at[1, 0],
            recv_sem=left_recv.at[u, col, b],
            device_id=(row, up),
            device_id_type=MESH,
        ).wait_recv()

    far_y = (y + 2) % ny
    far, far_partner = far_y * 2 + xh, far_y * 2 + 1 - xh
    up_partner, down_partner = up_y * 2 + 1 - xh, down_y * 2 + 1 - xh
    from_down, from_up = down_y * 2, up_y * 2 + 1

    def first(u):
        if isinstance(u, int) and u == 0:

            @pl.when(ahead != 0)
            def _():
                wait_piece(u, col)

        elif isinstance(u, int) and u == 1:
            wait_piece(u, col)
        else:
            wait_half(u, 0)
            wait_half(u, 1)
        hand_on(u, col, up, 0).start()
        hand_on(u, col, down, 1).start()
        hand_on(u, col, partner, 2).start()

    def second(u):
        turn = u // 2 % 2
        wait_piece(u, up)
        wait_piece(u, down)
        hand_on(u, down * turn + up * (1 - turn), up * turn + down * (1 - turn), 3, 1).start()
        hand_on(u, up, partner, 4, 1).start()
        hand_on(u, down, partner, 5, 1).start()
        wait_piece(u, partner)
        hand_on(u, partner, up, 6, 0).start()
        hand_on(u, partner, down, 7, 0).start()

    def third(u):
        wait_piece(u, far, 1)
        hand_on(u, far, partner, 8, 1).start()

        @pl.when(xh == 0)
        def _():
            wait_piece(u, up_partner, 0)

        @pl.when(xh == 1)
        def _():
            wait_piece(u, down_partner, 0)

        hand_on(u, from_down, up, 9, 0).start()
        hand_on(u, from_up, down, 10, 0).start()

    def rest(u):
        @pl.when(xh == 1)
        def _():
            wait_piece(u, up_partner, 0)

        @pl.when(xh == 0)
        def _():
            wait_piece(u, down_partner, 0)

        wait_piece(u, up_partner, 1)
        wait_piece(u, down_partner, 1)
        wait_piece(u, far, 0)
        wait_piece(u, far_partner, 0)
        wait_piece(u, far_partner, 1)

    width = 256 if cols % 256 == 0 else BLOCK

    def products(u):

        @pl.loop(0, cols // width)
        def _(n):
            start = pl.multiple_of(n * width, width)
            l0 = left[u, :, :, 0].reshape(rows, depth)
            l1 = left[u, :, :, 1].reshape(rows, depth)
            r0 = right[0, :, pl.ds(start, width)]
            r1 = right[1, :, pl.ds(start, width)]
            square = jnp.dot(l0, r0, preferred_element_type=jnp.float32)
            tangent = jnp.dot(l0, r1, preferred_element_type=jnp.float32)
            tangent = tangent + jnp.dot(l1, r0, preferred_element_type=jnp.float32)
            for b in range(2):
                part[u, b, :, pl.ds(start, width)] = square[b * half : (b + 1) * half]
                part[u, b, :, pl.ds(cols + start, width)] = tangent[b * half : (b + 1) * half]

    def slot_of(way, h, d):
        return (way * 2 + h) * (nz // 2) + d - 1

    def values_copy(way, h, d):
        slot = slot_of(way, h, d)
        zn = (z + 1 + way * (nz - 2)) % nz
        return pltpu.make_async_remote_copy(
            src_ref=q_out.at[slot],
            dst_ref=q_in.at[slot],
            send_sem=q_send.at[slot],
            recv_sem=q_recv.at[slot],
            device_id=(zn * group + s, col),
            device_id_type=MESH,
        )

    def scales_copy(way, h, d):
        slot = slot_of(way, h, d)
        zn = (z + 1 + way * (nz - 2)) % nz
        return pltpu.make_async_remote_copy(
            src_ref=s_out.at[slot],
            dst_ref=s_in.at[slot],
            send_sem=s_send.at[slot],
            recv_sem=s_recv.at[slot],
            device_id=(zn * group + s, col),
            device_id_type=MESH,
        )

    def arrived(way, h, d):
        values_copy(way, h, d).wait_recv()
        scales_copy(way, h, d).wait_recv()

    def decoded(slot, lanes):
        return q_in[slot, :, lanes].astype(jnp.int32).astype(jnp.float32) * s_in[slot, :, lanes]

    def send_on(u, b, way, h, d, adding):
        slot = slot_of(way, h, d)
        if adding:
            arrived(way, h, d + 1)

        @pl.loop(0, 2 * cols // BLOCK)
        def _(j):
            lanes = pl.ds(pl.multiple_of(j * BLOCK, BLOCK), BLOCK)
            total = part[u, b, :, lanes]
            if adding:
                total = total + decoded(slot + 1, lanes)
            top = jnp.maximum(jnp.max(jnp.abs(total), axis=0, keepdims=True), FLOOR)
            q_out[slot, :, lanes] = jnp.round(total * (LEVELS / top)).astype(jnp.int32).astype(jnp.int16)
            s_out[slot, :, lanes] = top * (1.0 / LEVELS)

        values_copy(way, h, d).start()
        scales_copy(way, h, d).start()

    def ring_step(u):
        h, d = u % 2, nz // 2 - u // 2

        @pl.when(u < 4)
        def _():
            send_on(u, 1 - h, 1 - h, h, d, False)

        @pl.when(u >= 4)
        def _():
            send_on(u, 1 - h, 1 - h, h, d, True)

        send_on(u, h, h, h, d, True)

    def if_any(stage, u):
        pl.when(u < nz)(functools.partial(stage, u))

    onward(4, 0)
    first(0)
    second(0)
    first(1)
    onward(5, 0)
    onward(3, 0)
    second(1)
    onward(5, 1)
    onward(3, 1)
    third(1)
    onward(6, 0)
    onward(2, 0)
    onward(6, 1)
    onward(2, 1)
    first(2)
    rest(1)
    products(1)
    send_on(1, 0, 0, 0, nz // 2, False)
    send_on(1, 1, 1, 1, nz // 2, False)
    onward(7, 0)
    onward(1, 0)
    onward(7, 1)
    onward(1, 1)
    second(2)
    first(3)
    third(0)

    @pl.loop(2, nz)
    def _(u):
        third(u)
        if_any(second, u + 1)
        if_any(first, u + 2)
        rest(u)
        products(u)
        ring_step(u)

    rest(0)
    products(0)

    for h in range(2):
        arrived(0, h, 1)
        arrived(1, h, 1)
        for which in range(2):
            for j in range(cols // BLOCK):
                lanes = slice(which * cols + j * BLOCK, which * cols + (j + 1) * BLOCK)
                total = part[0, h, :, lanes] + decoded(slot_of(0, h, 1), lanes)
                total = total + decoded(slot_of(1, h, 1), lanes)
                total = total.reshape(nc, thin, BLOCK)
                per_block = BLOCK // (2 * thin)
                for i in range(nc // per_block):
                    keep_it = keep[i, j].astype(jnp.float32)
                    span = slice(i * per_block, (i + 1) * per_block)
                    stage[which, span, h, :, j * BLOCK : (j + 1) * BLOCK] = (total[span] * keep_it).astype(jnp.bfloat16)

    stores = []
    for which, out in enumerate((out_square, out_tangent)):
        store = pltpu.make_async_copy(stage.at[which], out, store_sem.at[which])
        store.start()
        stores.append(store)

    for k in range(1, nc):
        scatter(k).wait_send()
    for i in range(1, nz):
        for h in range(1 if i == nz // 2 else 2):
            to_plane(i, h).wait_send()

    def sent(u):
        for k in range(11):
            hand_on(u, col, up, k, None if k < 3 else 0).wait_send()

    pl.loop(0, nz)(sent)

    for way in range(2):
        for h in range(2):
            for d in range(1, nz // 2 + (1 if way == h else 0)):
                values_copy(way, h, d).wait_send()
                scales_copy(way, h, d).wait_send()
    for store in stores:
        store.wait()


def hand_out(square, tangent, out_square, out_tangent):
    out_square[...] = square[...]
    out_tangent[...] = tangent[...]


def per_device(nz, nc, group, x0_rows, x1_rows, x0_cols, x1_cols, m0_rows, m1_rows, m0_cols, m1_cols, keep):
    rows = x0_rows.shape[0]
    depth, cols = x0_cols.shape
    thin, half, slots = rows // (2 * nc), rows // 2, 2 * nz
    x0_rows, x1_rows = (x.reshape(nc, 2, thin, -1) for x in (x0_rows, x1_rows))
    hbm = pl.BlockSpec(memory_space=pl.ANY)
    smem = pl.BlockSpec(memory_space=pltpu.SMEM)
    dma = pltpu.SemaphoreType.DMA
    out = jax.ShapeDtypeStruct((nc, 2, thin, cols), jnp.bfloat16)
    square, tangent = pl.pallas_call(
        functools.partial(kernel, group, nz, nc),
        out_shape=(out, out),
        in_specs=[hbm] * 4 + [smem] * 5,
        out_specs=(hbm, hbm),
        scratch_shapes=[
            pltpu.VMEM((nc, 2, 2, thin, depth), jnp.bfloat16),
            pltpu.VMEM((nc, 2, 2, thin, depth), jnp.bfloat16),
            pltpu.VMEM((nz, 2, nc, 2, thin, depth), jnp.bfloat16),
            pltpu.VMEM((2, depth, cols), jnp.bfloat16),
            pltpu.VMEM((nz, 2, half, 2 * cols), jnp.float32),
            pltpu.VMEM((slots, half, 2 * cols), jnp.int16),
            pltpu.VMEM((slots, half, 2 * cols), jnp.int16),
            pltpu.VMEM((slots, 1, 2 * cols), jnp.float32),
            pltpu.VMEM((slots, 1, 2 * cols), jnp.float32),
            pltpu.VMEM((2, nc, 2, thin, cols), jnp.bfloat16),
            dma((2,)),
            dma((2,)),
            dma((nc,)),
            dma((nc,)),
            dma((nz, 2)),
            dma((nz, nc, 2)),
            dma((nz, 11)),
            dma((slots,)),
            dma((slots,)),
            dma((slots,)),
            dma((slots,)),
            dma((2,)),
        ],
        compiler_params=pltpu.CompilerParams(
            collective_id=0, has_side_effects=True, vmem_limit_bytes=56 * 1024 * 1024
        ),
        name="window_kernel",
    )(x0_rows, x1_rows, x0_cols, x1_cols, m0_rows, m1_rows, m0_cols, m1_cols, keep)
    return pl.pallas_call(
        hand_out,
        out_shape=(jax.ShapeDtypeStruct((rows, cols), jnp.bfloat16),) * 2,
        name="hand_out",
    )(square.reshape(rows, cols), tangent.reshape(rows, cols))


def solution(mesh):
    nc = mesh.shape["col"]
    nz = 8
    group = mesh.shape["row"] // nz
    return jax.shard_map(
        functools.partial(per_device, nz, nc, group),
        mesh=mesh,
        in_specs=(P("row", "col"),) * 9,
        out_specs=(P("row", "col"), P("row", "col")),
        check_vma=False,
    )
```
